32 devices in a mesh: batch: 4 (over y, core), pts: 8 (over z, x).
Axes of the slice: x: 2, y: 2, z: 4, core: 2. Of those that a mesh axis runs over, the one named last changes fastest.
Arguments:
- mesh_attributes: bfloat16 [32768, 512], P(('batch', 'pts')), parts along dimension 0, may hold values from -12 to 12
- occupied_vertices_tally: int32 [32], P(('batch', 'pts')), parts along dimension 0, may hold values from 512 to 1024, as said below
- vertex_content_matrix: bfloat16 [4, 512, 512], replicated, may hold values from -0.25 to 0.25
- vertex_partition_matrix: bfloat16 [4, 512, 512], replicated, may hold values from -0.25 to 0.25
- partition_affinity_matrix: bfloat16 [4, 8, 64, 64], replicated, may hold values from -0.75 to 0.75
- softmax_sharpness: float32 [4, 8], replicated, may hold values from 0.02 to 1
- partition_asking_matrix: bfloat16 [4, 64, 64], replicated, may hold values from -0.75 to 0.75
- partition_matching_matrix: bfloat16 [4, 64, 64], replicated, may hold values from -0.75 to 0.75
- partition_content_matrix: bfloat16 [4, 64, 64], replicated, may hold values from -0.75 to 0.75
- attention_result_matrix: bfloat16 [4, 512, 512], replicated, may hold values from -0.25 to 0.25
- widening_matrix: bfloat16 [4, 512, 512], replicated, may hold values from -0.25 to 0.25
- contracting_matrix: bfloat16 [4, 512, 512], replicated, may hold values from -0.25 to 0.25
Outputs:
- result: bfloat16 [32768, 512], P(('batch', 'pts')), parts along dimension 0
The draws below stay inside these ranges and needn't reach their ends.
There are 4 independent parts, one for each index of `batch`. The reference program is written for one: setup_inputs(seed, part) draws one part's arguments, and reference() takes and returns one part's arrays. A program takes and returns all parts, laid end to end along the dimension named above; an argument that names none is the same for every part. Nothing has to cross between parts.
Inputs may be any that keep to these rules, and one draw needn't show every extreme that they name: `occupied_vertices_tally`: the shard of some index holds 1024 live points in every draw.
All inputs are finite; a program needn't handle non-finite values.
Results may differ from the reference program's by a relative error of at most 0.0055.
Values sent between devices are 32-bit elements; how exact they have to be, the bound alone decides.
A program may use at most 64 MiB of HBM per device.

```python
import jax
import jax.numpy as jnp
from jax import lax

D = 512
H = 8
DH = 64
G = 64
FF = 512
LAYERS = 4
PTS_DEV = 1024
POINTS = 8192
N_PTS = 8


def draw_mesh_attributes(key, part):
    keys = jax.random.split(jax.random.fold_in(key, 11), 5)
    position = jnp.arange(POINTS, dtype=jnp.float32) / POINTS
    freqs = jnp.arange(1, 5, dtype=jnp.float32)
    phase = jax.random.uniform(keys[0], (4,), minval=0.0, maxval=6.2831853)
    basis = jnp.sin(6.2831853 * position[:, None] * freqs[None, :] + phase[None, :])
    direction = jax.random.normal(keys[1], (4, D), dtype=jnp.float32)
    smooth = jnp.dot(basis, direction, precision=lax.Precision.HIGHEST)
    regional = jnp.repeat(3.0 * jax.random.normal(keys[4], (N_PTS, D), dtype=jnp.float32), PTS_DEV, axis=0)
    field = jax.random.normal(keys[2], (POINTS, D), dtype=jnp.float32) + smooth + regional
    return jnp.clip(field, -12.0, 12.0).astype(jnp.bfloat16)


def draw_occupied_vertices_tally(key, part):
    keys = jax.random.split(jax.random.fold_in(key, 23), 2)
    drawn = jax.random.randint(keys[0], (N_PTS,), PTS_DEV // 2, PTS_DEV + 1)
    filled = jax.random.randint(keys[1], (), 0, N_PTS)
    return jnp.where(jnp.arange(N_PTS) == filled, PTS_DEV, drawn).astype(jnp.int32)


def draw_softmax_sharpness(key, part):
    lowest = 0.12
    uniform_draw = jax.random.uniform(jax.random.fold_in(key, 37), (LAYERS, H), dtype=jnp.float32)
    return jnp.exp(jnp.log(lowest) * (1.0 - uniform_draw))


def bell_draw(stream_key, extent, width, most, kind=jnp.bfloat16):
    result = jax.random.normal(stream_key, extent, jnp.float32) * width
    return jnp.minimum(jnp.maximum(result, -most), most).astype(kind)


def setup_inputs(seed: int = 0, part: int = 0) -> dict:
    seeds = jax.random.split(jax.random.key(seed), 13)
    own_keys = jax.random.split(jax.random.fold_in(seeds[12], part), 13)
    mesh_attributes = draw_mesh_attributes(jax.random.fold_in(jax.random.fold_in(seeds[12], part), 71), part)
    occupied_vertices_tally = draw_occupied_vertices_tally(jax.random.fold_in(jax.random.fold_in(seeds[12], part), 71), part)
    vertex_content_matrix = bell_draw(seeds[2], (LAYERS, D, D), D ** -0.5, 0.25)
    vertex_partition_matrix = bell_draw(seeds[3], (LAYERS, D, D), D ** -0.5, 0.25)
    partition_affinity_matrix = bell_draw(seeds[4], (LAYERS, H, DH, G), DH ** -0.5, 0.75)
    softmax_sharpness = draw_softmax_sharpness(jax.random.fold_in(seeds[12], 71), part)
    partition_asking_matrix = bell_draw(seeds[6], (LAYERS, DH, DH), DH ** -0.5, 0.75)
    partition_matching_matrix = bell_draw(seeds[7], (LAYERS, DH, DH), DH ** -0.5, 0.75)
    partition_content_matrix = bell_draw(seeds[8], (LAYERS, DH, DH), DH ** -0.5, 0.75)
    attention_result_matrix = bell_draw(seeds[9], (LAYERS, D, D), D ** -0.5, 0.25)
    widening_matrix = bell_draw(seeds[10], (LAYERS, D, FF), D ** -0.5, 0.25)
    contracting_matrix = bell_draw(seeds[11], (LAYERS, FF, D), FF ** -0.5, 0.25)
    return dict(mesh_attributes=mesh_attributes, occupied_vertices_tally=occupied_vertices_tally, vertex_content_matrix=vertex_content_matrix, vertex_partition_matrix=vertex_partition_matrix, partition_affinity_matrix=partition_affinity_matrix, softmax_sharpness=softmax_sharpness, partition_asking_matrix=partition_asking_matrix, partition_matching_matrix=partition_matching_matrix, partition_content_matrix=partition_content_matrix, attention_result_matrix=attention_result_matrix, widening_matrix=widening_matrix, contracting_matrix=contracting_matrix)


def layer_norm(stream):
    average = lax.optimization_barrier(jnp.mean(stream, axis=-1, keepdims=True))
    centred = stream - average
    variance = lax.optimization_barrier(jnp.mean(centred * centred, axis=-1, keepdims=True))
    return centred * lax.rsqrt(variance + 1e-05)

def attend_slices(tokens, partition_asking_matrix, partition_matching_matrix, partition_content_matrix):
    highest = lax.Precision.HIGHEST
    queries = jnp.einsum('hgd,de->hge', tokens, partition_asking_matrix.astype(jnp.float32), precision=highest)
    key_rows = jnp.einsum('hgd,de->hge', tokens, partition_matching_matrix.astype(jnp.float32), precision=highest)
    val_rows = jnp.einsum('hgd,de->hge', tokens, partition_content_matrix.astype(jnp.float32), precision=highest)
    scores = jnp.einsum('hgd,hkd->hgk', queries, key_rows, precision=highest) * queries.shape[-1] ** (-0.5)
    attn_probs = jax.nn.softmax(scores, axis=-1)
    return jnp.einsum('hgk,hkd->hgd', attn_probs, val_rows, precision=highest)

def reference(mesh_attributes, occupied_vertices_tally, vertex_content_matrix, vertex_partition_matrix, partition_affinity_matrix, softmax_sharpness, partition_asking_matrix, partition_matching_matrix, partition_content_matrix, attention_result_matrix, widening_matrix, contracting_matrix):
    points = mesh_attributes.shape[0]
    live = jnp.arange(PTS_DEV, dtype=jnp.int32)[None, :] < occupied_vertices_tally[:, None]
    live_mask = live.reshape(points).astype(jnp.float32)
    stream = mesh_attributes.astype(jnp.float32)
    for stacked_level_index in range(LAYERS):
        normed = layer_norm(stream).astype(jnp.bfloat16)
        values = jnp.dot(normed, vertex_content_matrix[stacked_level_index], preferred_element_type=jnp.float32).astype(jnp.bfloat16)
        slice_feats = jnp.dot(normed, vertex_partition_matrix[stacked_level_index], preferred_element_type=jnp.float32).astype(jnp.bfloat16)
        partition_raw_affinities = jnp.einsum('phd,hdg->phg', slice_feats.reshape(points, H, DH).astype(jnp.float32), partition_affinity_matrix[stacked_level_index].astype(jnp.float32))
        partition_raw_affinities = partition_raw_affinities / softmax_sharpness[stacked_level_index][None, :, None]
        weights = (jax.nn.softmax(partition_raw_affinities, axis=-1) * live_mask[:, None, None]).astype(jnp.bfloat16)
        numerator = jnp.einsum('phg,phd->hgd', weights.astype(jnp.float32), values.reshape(points, H, DH).astype(jnp.float32))
        mass = lax.optimization_barrier(jnp.sum(weights.astype(jnp.float32), axis=0))
        tokens = numerator / (mass + 1e-05)[:, :, None]
        attended = attend_slices(tokens, partition_asking_matrix[stacked_level_index], partition_matching_matrix[stacked_level_index], partition_content_matrix[stacked_level_index]).astype(jnp.bfloat16)
        spread = jnp.einsum('phg,hgd->phd', weights.astype(jnp.float32), attended.astype(jnp.float32))
        spread = spread.reshape(points, D).astype(jnp.bfloat16)
        stream = stream + jnp.dot(spread, attention_result_matrix[stacked_level_index], preferred_element_type=jnp.float32)
        normed = layer_norm(stream).astype(jnp.bfloat16)
        hidden = jax.nn.gelu(jnp.dot(normed, widening_matrix[stacked_level_index], preferred_element_type=jnp.float32)).astype(jnp.bfloat16)
        stream = stream + jnp.dot(hidden, contracting_matrix[stacked_level_index], preferred_element_type=jnp.float32)
    return (stream * live_mask[:, None]).astype(jnp.bfloat16)
```

```python
import functools

import jax
import jax.numpy as jnp
from jax import lax
from jax.experimental import pallas as pl
from jax.experimental.pallas import tpu as pltpu
from jax.sharding import PartitionSpec as P

F32 = jnp.float32
BF16 = jnp.bfloat16
LOG2E = 1.4426950408889634
HIGHEST = lax.Precision.HIGHEST


def dot(a, b, ca=1, cb=0, precision=None):
    return lax.dot_general(
        a, b, (((ca,), (cb,)), ((), ())), preferred_element_type=F32, precision=precision
    )


def norm_columns(s):
    scale = 1.0 / s.shape[0]
    centred = s - jnp.sum(s, axis=0, keepdims=True) * scale
    variance = jnp.sum(centred * centred, axis=0, keepdims=True) * scale
    return (centred * lax.rsqrt(variance + 1e-05)).astype(BF16)


def gelu(x):
    inner = x * (0.7978845608028654 + (0.7978845608028654 * 0.044715) * (x * x))
    half = 0.5 * x
    return half + half * jnp.tanh(inner)


def kernel(
    n,
    chunk,
    tally_ref,
    sharp_ref,
    x_ref,
    aff_ref,
    ask_ref,
    match_ref,
    cont_ref,
    wv_hbm,
    wp_hbm,
    wo_hbm,
    ww_hbm,
    wc_hbm,
    out_ref,
    wv,
    wp,
    wo,
    ww,
    wc,
    stream,
    wts,
    vals,
    fold,
    wt,
    mt,
    rs_send,
    rs_recv,
    ag_send,
    ag_recv,
    w_sem,
    rs_ssem,
    rs_rsem,
    ag_ssem,
    ag_rsem,
):
    layers, heads, dh, groups = aff_ref.shape
    points, feats = x_ref.shape
    hg = heads * groups
    owners = min(n, heads)
    stride = n // owners
    hpo = heads // owners
    half = dh // 2
    me = lax.axis_index("pts")
    my_owner = me // stride
    is_owner = lax.rem(me, stride) == 0
    chunks = points // chunk

    copies = []
    for j, (src, dst) in enumerate(
        ((wp_hbm, wp), (wv_hbm, wv), (wo_hbm, wo), (ww_hbm, ww), (wc_hbm, wc))
    ):
        copies.append((src, dst, j))

    def weight_copy(j, l):
        src, dst, k = copies[j]
        return pltpu.make_async_copy(src.at[l], dst.at[l], w_sem.at[k, l])

    for l in range(layers):
        for j in range(5):
            weight_copy(j, l).start()

    barrier = pltpu.get_barrier_semaphore()
    for k in range(1, n):
        pl.semaphore_signal(
            barrier,
            inc=1,
            device_id={"pts": lax.rem(me + k, n)},
            device_id_type=pl.DeviceIdType.MESH,
        )
    pl.semaphore_wait(barrier, n - 1)

    tally = tally_ref[0]

    def live(c):
        at = lax.broadcasted_iota(jnp.int32, (1, chunk), 1) + c * chunk
        return at < tally

    def prepare(l):
        slot = lax.rem(l, 2)
        for j in range(5):
            weight_copy(j, l).wait()
        zero = jnp.zeros((groups, dh), BF16)
        for p in range(heads // 2):
            top = aff_ref[l, 2 * p].astype(F32).T.astype(BF16)
            low = aff_ref[l, 2 * p + 1].astype(F32).T.astype(BF16)
            pair = jnp.concatenate(
                [jnp.concatenate([top, zero], 1), jnp.concatenate([zero, low], 1)], 0
            )
            both = dot(pair, wp[l, :, 2 * p * dh : 2 * (p + 1) * dh], 1, 1)
            for i in range(2):
                h = 2 * p + i
                fold[h * groups : (h + 1) * groups, :] = (
                    both[i * groups : (i + 1) * groups] * (LOG2E / sharp_ref[l, h])
                ).astype(BF16)
        for j, w in enumerate((wv, wo, ww, wc)):
            wt[slot, j] = w[l].T
        mt[slot] = dot(
            match_ref[l].astype(F32), ask_ref[l].astype(F32), 1, 1, HIGHEST
        ) * (dh**-0.5)

    for c in range(chunks):
        at = slice(c * chunk, (c + 1) * chunk)
        stream[:, at] = x_ref[at, :].astype(F32).T
    for q in range(vals.shape[0]):
        vals[q, vals.shape[1] - 16 :, :] = jnp.ones((16, points), BF16)
    prepare(jnp.int32(0))

    quads = vals.shape[0]
    qh = heads // quads
    lane = lax.broadcasted_iota(jnp.int32, (half, 2 * groups), 1) < groups
    lane_mass = lax.broadcasted_iota(jnp.int32, (8, 2 * groups), 1) < groups

    def rs_copy(owner, source):
        return pltpu.make_async_remote_copy(
            src_ref=rs_send.at[pl.ds(owner * hpo, hpo)],
            dst_ref=rs_recv.at[source],
            send_sem=rs_ssem.at[owner],
            recv_sem=rs_rsem.at[source],
            device_id={"pts": owner * stride},
            device_id_type=pl.DeviceIdType.MESH,
        )

    def ag_copy(owner, target):
        return pltpu.make_async_remote_copy(
            src_ref=ag_send,
            dst_ref=ag_recv.at[pl.ds(owner * hpo, hpo)],
            send_sem=ag_ssem.at[target],
            recv_sem=ag_rsem.at[owner],
            device_id={"pts": target},
            device_id_type=pl.DeviceIdType.MESH,
        )

    def other_owners(body):
        for k in range(owners):
            owner = lax.rem(my_owner + k, owners)
            if stride == 1:
                if k:
                    body(owner)
            else:
                pl.when(owner * stride != me)(functools.partial(body, owner))

    def layer(l, carry):
        slot = lax.rem(l, 2)
        for c in range(chunks):
            at = slice(c * chunk, (c + 1) * chunk)
            normed = norm_columns(stream[:, at])
            logits = dot(fold[...], normed)
            keep = live(c)
            for h in range(heads):
                part = logits[h * groups : (h + 1) * groups]
                e = jnp.exp2(part - jnp.max(part, axis=0, keepdims=True))
                r = jnp.where(keep, 1.0 / jnp.sum(e, axis=0, keepdims=True), 0.0)
                wts[h * groups : (h + 1) * groups, at] = (e * r).astype(BF16)
            v = dot(wt[slot, 0], normed).astype(BF16)
            for q in range(quads):
                vals[q, : qh * dh, at] = v[q * qh * dh : (q + 1) * qh * dh]
        for q in range(quads):
            total = dot(vals[q], wts[q * qh * groups : (q + 1) * qh * groups, :], 1, 1)
            for i in range(qh):
                h = q * qh + i
                cols = slice((i // 2) * 2 * groups, (i // 2 + 1) * 2 * groups)
                top = total[i * dh : i * dh + half, cols]
                low = total[i * dh + half : (i + 1) * dh, cols]
                mass = total[qh * dh : qh * dh + 8, cols]
                turned = pltpu.roll(mass, groups, 1)
                if i % 2 == 0:
                    rs_send[h, :half] = jnp.where(lane, top, pltpu.roll(low, groups, 1))
                    rs_send[h, half:] = jnp.where(lane_mass, mass, turned)
                else:
                    rs_send[h, :half] = jnp.where(lane, pltpu.roll(top, groups, 1), low)
                    rs_send[h, half:] = jnp.where(lane_mass, turned, mass)
        other_owners(lambda owner: rs_copy(owner, me).start())

        @pl.when(l + 1 < layers)
        def _():
            prepare_next(l)

        def attend():
            for k in range(1, n):
                rs_copy(my_owner, lax.rem(me + k, n)).wait_recv()
            for i in range(hpo):
                acc = rs_send[my_owner * hpo + i]
                for k in range(1, n):
                    acc = acc + rs_recv[lax.rem(me + k, n), i]
                packed = acc[:half] / (acc[half : half + 1] + 1e-05)
                tokens = jnp.concatenate([packed[:, :groups], packed[:, groups:]], 0)
                u = dot(mt[slot], tokens, 1, 0, HIGHEST)
                v = dot(cont_ref[l].astype(F32).T, tokens, 1, 0, HIGHEST)
                scores = dot(tokens.T, u, 1, 0, HIGHEST)
                e = jnp.exp(scores - jnp.max(scores, axis=0, keepdims=True))
                probs = e / jnp.sum(e, axis=0, keepdims=True)
                att = dot(v, probs, 1, 0, HIGHEST)
                ag_send[i] = jnp.concatenate([att[:half], att[half:]], 1)
            for k in range(1, n):
                ag_copy(my_owner, lax.rem(me + k, n)).start()
            for i in range(hpo):
                ag_recv[my_owner * hpo + i] = ag_send[i]

        if stride == 1:
            attend()
        else:
            pl.when(is_owner)(attend)

        other_owners(lambda owner: ag_copy(owner, me).wait_recv())

        mixes = []
        zero = jnp.zeros((2 * dh, 2 * groups), BF16)
        for p in range(heads // 2):
            even = ag_recv[2 * p]
            odd = ag_recv[2 * p + 1]
            block = jnp.concatenate(
                [
                    jnp.where(lane, even, 0.0),
                    jnp.where(lane, pltpu.roll(even, groups, 1), 0.0),
                    jnp.where(lane, 0.0, pltpu.roll(odd, groups, 1)),
                    jnp.where(lane, 0.0, odd),
                ],
                0,
            ).astype(BF16)
            mixes.append(
                dot(wt[slot, 1, :, 2 * p * dh : 2 * (p + 1) * dh], block).astype(BF16)
            )
        mix = jnp.concatenate(mixes, 1)
        for c in range(chunks):
            at = slice(c * chunk, (c + 1) * chunk)
            s = stream[:, at] + dot(mix, wts[:, at])
            hidden = gelu(dot(wt[slot, 2], norm_columns(s))).astype(BF16)
            stream[:, at] = s + dot(wt[slot, 3], hidden)

        other_owners(lambda owner: rs_copy(owner, me).wait_send())

        def sent():
            for k in range(1, n):
                ag_copy(my_owner, lax.rem(me + k, n)).wait_send()

        if stride == 1:
            sent()
        else:
            pl.when(is_owner)(sent)
        return carry

    def prepare_next(l):
        prepare(l + 1)

    lax.fori_loop(0, layers, layer, 0)

    for c in range(chunks):
        at = slice(c * chunk, (c + 1) * chunk)
        out_ref[at, :] = jnp.where(live(c), stream[:, at], 0.0).T.astype(BF16)


def per_device(n, x, tally, wv, wp, aff, sharp, ask, match, cont, wo, ww, wc):
    points, feats = x.shape
    layers, heads, dh, groups = aff.shape
    owners = min(n, heads)
    hpo = heads // owners
    quads = max(1, heads // 4)
    chunk = min(points, 256)
    vmem = pl.BlockSpec(memory_space=pltpu.VMEM)
    smem = pl.BlockSpec(memory_space=pltpu.SMEM)
    hbm = pl.BlockSpec(memory_space=pl.ANY)
    dma = pltpu.SemaphoreType.DMA
    return pl.pallas_call(
        functools.partial(kernel, n, chunk),
        out_shape=jax.ShapeDtypeStruct((points, feats), BF16),
        in_specs=[smem, smem] + [vmem] * 5 + [hbm] * 5,
        out_specs=vmem,
        scratch_shapes=[
            pltpu.VMEM(wv.shape, BF16),
            pltpu.VMEM(wp.shape, BF16),
            pltpu.VMEM(wo.shape, BF16),
            pltpu.VMEM(ww.shape, BF16),
            pltpu.VMEM(wc.shape, BF16),
            pltpu.VMEM((feats, points), F32),
            pltpu.VMEM((heads * groups, points), BF16),
            pltpu.VMEM((quads, heads // quads * dh + 16, points), BF16),
            pltpu.VMEM((heads * groups, feats), BF16),
            pltpu.VMEM((2, 4) + wv.shape[1:], BF16),
            pltpu.VMEM((2, dh, dh), F32),
            pltpu.VMEM((heads, dh // 2 + 8, 2 * groups), F32),
            pltpu.VMEM((n, hpo, dh // 2 + 8, 2 * groups), F32),
            pltpu.VMEM((hpo, dh // 2, 2 * groups), F32),
            pltpu.VMEM((heads, dh // 2, 2 * groups), F32),
            dma((5, layers)),
            dma((owners,)),
            dma((n,)),
            dma((n,)),
            dma((owners,)),
        ],
        compiler_params=pltpu.CompilerParams(
            collective_id=0, has_side_effects=True, vmem_limit_bytes=60 * 1024 * 1024
        ),
    )(tally, sharp, x, aff, ask, match, cont, wv, wp, wo, ww, wc)


def solution(mesh):
    rows = P(("batch", "pts"), None)
    placed = (rows, P(("batch", "pts"))) + (P(),) * 10
    return jax.shard_map(
        functools.partial(per_device, mesh.shape["pts"]),
        mesh=mesh,
        in_specs=placed,
        out_specs=rows,
        check_vma=False,
    )
```

```python
import functools

import jax
import jax.numpy as jnp
from jax import lax
from jax.experimental import pallas as pl
from jax.experimental.pallas import tpu as pltpu
from jax.sharding import PartitionSpec as P

F32 = jnp.float32
BF16 = jnp.bfloat16
LOG2E = 1.4426950408889634
HIGHEST = lax.Precision.HIGHEST


def dot(a, b, ca=1, cb=0, precision=None):
    return lax.dot_general(
        a, b, (((ca,), (cb,)), ((), ())), preferred_element_type=F32, precision=precision
    )


def norm_columns(s):
    scale = 1.0 / s.shape[0]
    centred = s - jnp.sum(s, axis=0, keepdims=True) * scale
    variance = jnp.sum(centred * centred, axis=0, keepdims=True) * scale
    return (centred * lax.rsqrt(variance + 1e-05)).astype(BF16)


def gelu(x):
    inner = x * (0.7978845608028654 + (0.7978845608028654 * 0.044715) * (x * x))
    half = 0.5 * x
    return half + half * jnp.tanh(inner)


def kernel(
    n,
    chunk,
    tally_ref,
    sharp_ref,
    x_ref,
    aff_ref,
    ask_ref,
    match_ref,
    cont_ref,
    wv_hbm,
    wp_hbm,
    wo_hbm,
    ww_hbm,
    wc_hbm,
    out_ref,
    wv,
    wp,
    wo,
    ww,
    wc,
    stream,
    normed,
    wts,
    vals,
    comb,
    wt,
    x_buf,
    mt,
    rs_send,
    rs_recv,
    ag_send,
    ag_recv,
    x_sem,
    w_sem,
    rs_ssem,
    rs_rsem,
    ag_ssem,
    ag_rsem,
):
    layers, heads, dh, groups = aff_ref.shape
    points, feats = x_ref.shape
    owners = min(n, heads)
    stride = n // owners
    hpo = heads // owners
    half = dh // 2
    me = lax.axis_index("pts")
    my_owner = me // stride
    is_owner = lax.rem(me, stride) == 0
    chunks = points // chunk

    copies = []
    for j, (src, dst) in enumerate(
        ((wp_hbm, wp), (wv_hbm, wv), (wo_hbm, wo), (ww_hbm, ww), (wc_hbm, wc))
    ):
        copies.append((src, dst, j))

    def weight_copy(j, l):
        src, dst, k = copies[j]
        return pltpu.make_async_copy(src.at[l], dst.at[l], w_sem.at[k, l])

    def x_copy(c):
        rows = pl.ds(c * chunk, chunk)
        return pltpu.make_async_copy(x_ref.at[rows], x_buf.at[rows], x_sem.at[c])

    barrier = pltpu.get_barrier_semaphore()
    for k in range(1, n):
        pl.semaphore_signal(
            barrier,
            inc=1,
            device_id={"pts": lax.rem(me + k, n)},
            device_id_type=pl.DeviceIdType.MESH,
        )
    for c in range(chunks):
        x_copy(c).start()
    for j in range(5):
        weight_copy(j, 0).start()

    offsets = sorted(range(1, n), key=lambda k: min(k, n - k))

    tally = tally_ref[0]

    def live(c):
        at = lax.broadcasted_iota(jnp.int32, (1, chunk), 1) + c * chunk
        return at < tally

    def prepare(l):
        slot = lax.rem(l, 2)
        for j in range(5):
            weight_copy(j, l).wait()

        @pl.when(l + 1 < layers)
        def _():
            for j in range(5):
                weight_copy(j, l + 1).start()

        zero = jnp.zeros((groups, dh), BF16)
        for p in range(heads // 2):
            top = aff_ref[l, 2 * p].astype(F32).T.astype(BF16)
            low = aff_ref[l, 2 * p + 1].astype(F32).T.astype(BF16)
            pair = jnp.concatenate(
                [jnp.concatenate([top, zero], 1), jnp.concatenate([zero, low], 1)], 0
            )
            both = dot(pair, wp[l, :, 2 * p * dh : 2 * (p + 1) * dh], 1, 1)
            for i in range(2):
                h = 2 * p + i
                row = (h % qh) * groups
                comb[h // qh, row : row + groups, :] = (
                    both[i * groups : (i + 1) * groups] * (LOG2E / sharp_ref[l, h])
                ).astype(BF16)
        turned = wv[l].T
        for q in range(quads):
            comb[q, qh * groups :, :] = turned[q * qh * dh : (q + 1) * qh * dh]
        for j, w in enumerate((wo, ww, wc)):
            wt[slot, j] = w[l].T
        mt[slot] = dot(
            match_ref[l].astype(F32), ask_ref[l].astype(F32), 1, 1, HIGHEST
        ) * (dh**-0.5)

    quads = vals.shape[0]
    qh = heads // quads

    def cols_of(c):
        return slice(c * chunk, (c + 1) * chunk)

    for q in range(quads):
        vals[q, vals.shape[1] - 16 :, :] = jnp.ones((16, points), BF16)
    for c in range(chunks):
        x_copy(c).wait()
        s = x_buf[cols_of(c), :].astype(F32).T
        stream[:, cols_of(c)] = s
        normed[:, cols_of(c)] = norm_columns(s)
    prepare(jnp.int32(0))
    pl.semaphore_wait(barrier, n - 1)

    lane = lax.broadcasted_iota(jnp.int32, (half, 2 * groups), 1) < groups
    lane_mass = lax.broadcasted_iota(jnp.int32, (8, 2 * groups), 1) < groups

    def rs_copy(owner, source):
        return pltpu.make_async_remote_copy(
            src_ref=rs_send.at[pl.ds(owner * hpo, hpo), pl.ds(0, half + 1)],
            dst_ref=rs_recv.at[source, pl.ds(0, hpo), pl.ds(0, half + 1)],
            send_sem=rs_ssem.at[owner],
            recv_sem=rs_rsem.at[source],
            device_id={"pts": owner * stride},
            device_id_type=pl.DeviceIdType.MESH,
        )

    def ag_copy(owner, target):
        return pltpu.make_async_remote_copy(
            src_ref=ag_send,
            dst_ref=ag_recv.at[pl.ds(owner * hpo, hpo)],
            send_sem=ag_ssem.at[target],
            recv_sem=ag_rsem.at[owner],
            device_id={"pts": target},
            device_id_type=pl.DeviceIdType.MESH,
        )

    def other_owners(body, low=0, high=owners):
        order = sorted(range(owners), key=lambda k: min(k, owners - k))
        for k in order:
            owner = lax.rem(my_owner + k, owners)
            if stride == 1 and k == 0:
                continue
            if stride == 1 and (low, high) == (0, owners):
                body(owner)
            else:
                here = (owner >= low) & (owner < high) & (owner * stride != me)
                pl.when(here)(functools.partial(body, owner))

    def layer(l, carry):
        slot = lax.rem(l, 2)

        def product(q, c):
            return dot(comb[q], normed[:, cols_of(c)])

        def weigh(q, c, prod):
            keep = live(c)
            for i in range(qh):
                part = prod[i * groups : (i + 1) * groups]
                e = jnp.exp2(part - jnp.max(part, axis=0, keepdims=True))
                r = jnp.where(keep, 1.0 / jnp.sum(e, axis=0, keepdims=True), 0.0)
                row = (q * qh + i) * groups
                wts[row : row + groups, cols_of(c)] = (e * r).astype(BF16)
            vals[q, : qh * dh, cols_of(c)] = prod[qh * groups :].astype(BF16)

        def reduce_quad(q):
            total = dot(vals[q], wts[q * qh * groups : (q + 1) * qh * groups, :], 1, 1)
            for i in range(qh):
                h = q * qh + i
                cols = slice((i // 2) * 2 * groups, (i // 2 + 1) * 2 * groups)
                top = total[i * dh : i * dh + half, cols]
                low = total[i * dh + half : (i + 1) * dh, cols]
                mass = total[qh * dh : qh * dh + 8, cols]
                turned = pltpu.roll(mass, groups, 1)
                if i % 2 == 0:
                    rs_send[h, :half] = jnp.where(lane, top, pltpu.roll(low, groups, 1))
                    rs_send[h, half:] = jnp.where(lane_mass, mass, turned)
                else:
                    rs_send[h, :half] = jnp.where(lane, pltpu.roll(top, groups, 1), low)
                    rs_send[h, half:] = jnp.where(lane_mass, turned, mass)
            other_owners(
                lambda owner: rs_copy(owner, me).start(),
                q * qh // hpo,
                (q + 1) * qh // hpo,
            )

        for q in range(quads):
            prod = product(q, 0)
            for c in range(chunks):
                later = product(q, c + 1) if c + 1 < chunks else None
                weigh(q, c, prod)
                prod = later
            if qh % hpo == 0:
                reduce_quad(q)

        @pl.when(l + 1 < layers)
        def _():
            prepare_next(l)

        def attend():
            for k in range(1, n):
                rs_copy(my_owner, lax.rem(me + k, n)).wait_recv()
            for i in range(hpo):
                acc = rs_send[my_owner * hpo + i]
                for k in range(1, n):
                    acc = acc + rs_recv[lax.rem(me + k, n), i]
                packed = acc[:half] / (acc[half : half + 1] + 1e-05)
                tokens = jnp.concatenate([packed[:, :groups], packed[:, groups:]], 0)
                u = dot(mt[slot], tokens, 1, 0, HIGHEST)
                v = dot(cont_ref[l].astype(F32).T, tokens, 1, 0, HIGHEST)
                scores = dot(tokens.T, u, 1, 0, HIGHEST)
                e = jnp.exp(scores - jnp.max(scores, axis=0, keepdims=True))
                probs = e / jnp.sum(e, axis=0, keepdims=True)
                att = dot(v, probs, 1, 0, HIGHEST)
                ag_send[i] = jnp.concatenate([att[:half], att[half:]], 1)
            for k in offsets:
                ag_copy(my_owner, lax.rem(me + k, n)).start()
            for i in range(hpo):
                ag_recv[my_owner * hpo + i] = ag_send[i]

        if stride == 1:
            attend()
        else:
            pl.when(is_owner)(attend)

        other_owners(lambda owner: ag_copy(owner, me).wait_recv())

        mixes = []
        zero = jnp.zeros((2 * dh, 2 * groups), BF16)
        for p in range(heads // 2):
            even = ag_recv[2 * p]
            odd = ag_recv[2 * p + 1]
            block = jnp.concatenate(
                [
                    jnp.where(lane, even, 0.0),
                    jnp.where(lane, pltpu.roll(even, groups, 1), 0.0),
                    jnp.where(lane, 0.0, pltpu.roll(odd, groups, 1)),
                    jnp.where(lane, 0.0, odd),
                ],
                0,
            ).astype(BF16)
            mixes.append(
                dot(wt[slot, 0, :, 2 * p * dh : 2 * (p + 1) * dh], block).astype(BF16)
            )
        mix = jnp.concatenate(mixes, 1)
        base, wide, hid = {}, {}, {}

        def stage(name, c):
            if not 0 <= c < chunks:
                return
            at = cols_of(c)
            if name == "mix":
                base[c] = stream[:, at] + dot(mix, wts[:, at])
            elif name == "widen":
                wide[c] = dot(wt[slot, 1], norm_columns(base[c]))
            elif name == "gelu":
                hid[c] = gelu(wide[c]).astype(BF16)
            elif name == "contract":
                s = base[c] + dot(wt[slot, 2], hid[c])
                stream[:, at] = s
                normed[:, at] = norm_columns(s)

        for t in range(chunks + 3):
            stage("mix", t)
            stage("gelu", t - 2)
            stage("widen", t - 1)
            stage("contract", t - 2)

        other_owners(lambda owner: rs_copy(owner, me).wait_send())

        def sent():
            for k in range(1, n):
                ag_copy(my_owner, lax.rem(me + k, n)).wait_send()

        if stride == 1:
            sent()
        else:
            pl.when(is_owner)(sent)
        return carry

    def prepare_next(l):
        prepare(l + 1)

    lax.fori_loop(0, layers, layer, 0)

    for c in range(chunks):
        at = slice(c * chunk, (c + 1) * chunk)
        out_ref[at, :] = jnp.where(live(c), stream[:, at], 0.0).T.astype(BF16)


def per_device(n, x, tally, wv, wp, aff, sharp, ask, match, cont, wo, ww, wc):
    points, feats = x.shape
    layers, heads, dh, groups = aff.shape
    owners = min(n, heads)
    hpo = heads // owners
    quads = max(1, heads // 4)
    chunk = min(points, 256)
    vmem = pl.BlockSpec(memory_space=pltpu.VMEM)
    smem = pl.BlockSpec(memory_space=pltpu.SMEM)
    hbm = pl.BlockSpec(memory_space=pl.ANY)
    dma = pltpu.SemaphoreType.DMA
    return pl.pallas_call(
        functools.partial(kernel, n, chunk),
        out_shape=jax.ShapeDtypeStruct((points, feats), BF16),
        in_specs=[smem, smem, hbm] + [vmem] * 4 + [hbm] * 5,
        out_specs=vmem,
        scratch_shapes=[
            pltpu.VMEM(wv.shape, BF16),
            pltpu.VMEM(wp.shape, BF16),
            pltpu.VMEM(wo.shape, BF16),
            pltpu.VMEM(ww.shape, BF16),
            pltpu.VMEM(wc.shape, BF16),
            pltpu.VMEM((feats, points), F32),
            pltpu.VMEM((feats, points), BF16),
            pltpu.VMEM((heads * groups, points), BF16),
            pltpu.VMEM((quads, heads // quads * dh + 16, points), BF16),
            pltpu.VMEM((quads, heads // quads * (groups + dh), feats), BF16),
            pltpu.VMEM((2, 3) + wv.shape[1:], BF16),
            pltpu.VMEM(x.shape, BF16),
            pltpu.VMEM((2, dh, dh), F32),
            pltpu.VMEM((heads, dh // 2 + 8, 2 * groups), F32),
            pltpu.VMEM((n, hpo, dh // 2 + 8, 2 * groups), F32),
            pltpu.VMEM((hpo, dh // 2, 2 * groups), F32),
            pltpu.VMEM((heads, dh // 2, 2 * groups), F32),
            dma((points // chunk,)),
            dma((5, layers)),
            dma((owners,)),
            dma((n,)),
            dma((n,)),
            dma((owners,)),
        ],
        compiler_params=pltpu.CompilerParams(
            collective_id=0, has_side_effects=True, vmem_limit_bytes=60 * 1024 * 1024
        ),
    )(tally, sharp, x, aff, ask, match, cont, wv, wp, wo, ww, wc)


def solution(mesh):
    rows = P(("batch", "pts"), None)
    placed = (rows, P(("batch", "pts"))) + (P(),) * 10
    return jax.shard_map(
        functools.partial(per_device, mesh.shape["pts"]),
        mesh=mesh,
        in_specs=placed,
        out_specs=rows,
        check_vma=False,
    )
```

```python
import functools

import jax
import jax.numpy as jnp
from jax import lax
from jax.experimental import pallas as pl
from jax.experimental.pallas import tpu as pltpu
from jax.sharding import PartitionSpec as P

F32 = jnp.float32
BF16 = jnp.bfloat16
LOG2E = 1.4426950408889634
HIGHEST = lax.Precision.HIGHEST


def dot(a, b, ca=1, cb=0, precision=None):
    return lax.dot_general(
        a, b, (((ca,), (cb,)), ((), ())), preferred_element_type=F32, precision=precision
    )


def norm_columns(s):
    scale = 1.0 / s.shape[0]
    centred = s - jnp.sum(s, axis=0, keepdims=True) * scale
    variance = jnp.sum(centred * centred, axis=0, keepdims=True) * scale
    return (centred * lax.rsqrt(variance + 1e-05)).astype(BF16)


def gelu(x):
    inner = x * (0.7978845608028654 + (0.7978845608028654 * 0.044715) * (x * x))
    half = 0.5 * x
    return half + half * jnp.tanh(inner)


def kernel(
    n,
    chunk,
    tally_ref,
    sharp_ref,
    x_ref,
    aff_ref,
    ask_ref,
    match_ref,
    cont_ref,
    wv_hbm,
    wp_hbm,
    wo_hbm,
    ww_hbm,
    wc_hbm,
    out_ref,
    wv,
    wp,
    wo,
    ww,
    wc,
    stream,
    normed,
    wts,
    vals,
    comb,
    wt,
    x_buf,
    mt,
    rs_send,
    rs_recv,
    ag_send,
    ag_recv,
    x_sem,
    w_sem,
    rs_ssem,
    rs_rsem,
    ag_ssem,
    ag_rsem,
):
    layers, heads, dh, groups = aff_ref.shape
    points, feats = x_ref.shape
    owners = min(n, heads)
    stride = n // owners
    hpo = heads // owners
    half = dh // 2
    me = lax.axis_index("pts")
    my_owner = me // stride
    is_owner = lax.rem(me, stride) == 0
    chunks = points // chunk

    copies = []
    for j, (src, dst) in enumerate(
        ((wp_hbm, wp), (wv_hbm, wv), (wo_hbm, wo), (ww_hbm, ww), (wc_hbm, wc))
    ):
        copies.append((src, dst, j))

    def weight_copy(j, l):
        src, dst, k = copies[j]
        return pltpu.make_async_copy(src.at[l], dst.at[l], w_sem.at[k, l])

    def x_copy(c):
        rows = pl.ds(c * chunk, chunk)
        return pltpu.make_async_copy(x_ref.at[rows], x_buf.at[rows], x_sem.at[c])

    barrier = pltpu.get_barrier_semaphore()
    for k in range(1, n):
        pl.semaphore_signal(
            barrier,
            inc=1,
            device_id={"pts": lax.rem(me + k, n)},
            device_id_type=pl.DeviceIdType.MESH,
        )
    for c in range(chunks):
        x_copy(c).start()
    for j in range(5):
        weight_copy(j, 0).start()

    offsets = sorted(range(1, n), key=lambda k: min(k, n - k))

    tally = tally_ref[0]

    def live(c):
        at = lax.broadcasted_iota(jnp.int32, (1, chunk), 1) + c * chunk
        return at < tally

    def prepare(l):
        slot = lax.rem(l, 2)
        for j in range(5):
            weight_copy(j, l).wait()

        @pl.when(l + 1 < layers)
        def _():
            for j in range(5):
                weight_copy(j, l + 1).start()

        zero = jnp.zeros((groups, dh), BF16)
        for p in range(heads // 2):
            top = aff_ref[l, 2 * p].astype(F32).T.astype(BF16)
            low = aff_ref[l, 2 * p + 1].astype(F32).T.astype(BF16)
            pair = jnp.concatenate(
                [jnp.concatenate([top, zero], 1), jnp.concatenate([zero, low], 1)], 0
            )
            both = dot(pair, wp[l, :, 2 * p * dh : 2 * (p + 1) * dh], 1, 1)
            for i in range(2):
                h = 2 * p + i
                row = (h % qh) * groups
                comb[h // qh, row : row + groups, :] = (
                    both[i * groups : (i + 1) * groups] * (LOG2E / sharp_ref[l, h])
                ).astype(BF16)
        turned = wv[l].T
        for q in range(quads):
            comb[q, qh * groups :, :] = turned[q * qh * dh : (q + 1) * qh * dh]
        for j, w in enumerate((wo, ww, wc)):
            wt[slot, j] = w[l].T
        mt[slot] = dot(
            match_ref[l].astype(F32), ask_ref[l].astype(F32), 1, 1, HIGHEST
        ) * (dh**-0.5)

    quads = vals.shape[0]
    qh = heads // quads

    def cols_of(c):
        return slice(c * chunk, (c + 1) * chunk)

    for q in range(quads):
        vals[q, vals.shape[1] - 16 :, :] = jnp.ones((16, points), BF16)
    for c in range(chunks):
        x_copy(c).wait()
        s = x_buf[cols_of(c), :].astype(F32).T
        stream[:, cols_of(c)] = s
        normed[:, cols_of(c)] = norm_columns(s)
    prepare(jnp.int32(0))
    pl.semaphore_wait(barrier, n - 1)

    lane = lax.broadcasted_iota(jnp.int32, (half, 2 * groups), 1) < groups
    lane_mass = lax.broadcasted_iota(jnp.int32, (8, 2 * groups), 1) < groups

    def rs_copy(owner, source):
        return pltpu.make_async_remote_copy(
            src_ref=rs_send.at[pl.ds(owner * hpo, hpo), pl.ds(0, half + 1)],
            dst_ref=rs_recv.at[source, pl.ds(0, hpo), pl.ds(0, half + 1)],
            send_sem=rs_ssem.at[owner],
            recv_sem=rs_rsem.at[source],
            device_id={"pts": owner * stride},
            device_id_type=pl.DeviceIdType.MESH,
        )

    def ag_copy(owner, target):
        return pltpu.make_async_remote_copy(
            src_ref=ag_send,
            dst_ref=ag_recv.at[pl.ds(owner * hpo, hpo)],
            send_sem=ag_ssem.at[target],
            recv_sem=ag_rsem.at[owner],
            device_id={"pts": target},
            device_id_type=pl.DeviceIdType.MESH,
        )

    def other_owners(body, low=0, high=owners):
        order = sorted(range(owners), key=lambda k: min(k, owners - k))
        for k in order:
            owner = lax.rem(my_owner + k, owners)
            if stride == 1 and k == 0:
                continue
            if stride == 1 and (low, high) == (0, owners):
                body(owner)
            else:
                here = (owner >= low) & (owner < high) & (owner * stride != me)
                pl.when(here)(functools.partial(body, owner))

    def layer(l, carry):
        slot = lax.rem(l, 2)

        def product(q, c):
            return dot(comb[q], normed[:, cols_of(c)])

        def weigh(q, c, prod):
            keep = live(c)
            for i in range(qh):
                part = prod[i * groups : (i + 1) * groups]
                e = jnp.exp2(part - jnp.max(part, axis=0, keepdims=True))
                r = jnp.where(keep, 1.0 / jnp.sum(e, axis=0, keepdims=True), 0.0)
                row = (q * qh + i) * groups
                wts[row : row + groups, cols_of(c)] = (e * r).astype(BF16)
            vals[q, : qh * dh, cols_of(c)] = prod[qh * groups :].astype(BF16)

        def reduce_quad(q):
            total = dot(vals[q], wts[q * qh * groups : (q + 1) * qh * groups, :], 1, 1)
            for i in range(qh):
                h = q * qh + i
                cols = slice((i // 2) * 2 * groups, (i // 2 + 1) * 2 * groups)
                top = total[i * dh : i * dh + half, cols]
                low = total[i * dh + half : (i + 1) * dh, cols]
                mass = total[qh * dh : qh * dh + 8, cols]
                turned = pltpu.roll(mass, groups, 1)
                if i % 2 == 0:
                    rs_send[h, :half] = jnp.where(lane, top, pltpu.roll(low, groups, 1))
                    rs_send[h, half:] = jnp.where(lane_mass, mass, turned)
                else:
                    rs_send[h, :half] = jnp.where(lane, pltpu.roll(top, groups, 1), low)
                    rs_send[h, half:] = jnp.where(lane_mass, turned, mass)
            other_owners(
                lambda owner: rs_copy(owner, me).start(),
                q * qh // hpo,
                (q + 1) * qh // hpo,
            )

        for q in range(quads):
            prod = product(q, 0)
            for c in range(chunks):
                later = product(q, c + 1) if c + 1 < chunks else None
                weigh(q, c, prod)
                prod = later
            if qh % hpo == 0:
                reduce_quad(q)

        @pl.when(l + 1 < layers)
        def _():
            prepare_next(l)

        def attend():
            for k in range(1, n):
                rs_copy(my_owner, lax.rem(me + k, n)).wait_recv()
            for i in range(hpo):
                acc = rs_send[my_owner * hpo + i]
                for k in range(1, n):
                    acc = acc + rs_recv[lax.rem(me + k, n), i]
                packed = acc[:half] / (acc[half : half + 1] + 1e-05)
                tokens = jnp.concatenate([packed[:, :groups], packed[:, groups:]], 0)
                u = dot(mt[slot], tokens, 1, 0, HIGHEST)
                v = dot(cont_ref[l].astype(F32).T, tokens, 1, 0, HIGHEST)
                scores = dot(tokens.T, u, 1, 0, HIGHEST)
                e = jnp.exp(scores - jnp.max(scores, axis=0, keepdims=True))
                probs = e / jnp.sum(e, axis=0, keepdims=True)
                att = dot(v, probs, 1, 0, HIGHEST)
                ag_send[i] = jnp.concatenate([att[:half], att[half:]], 1)
            for k in offsets:
                ag_copy(my_owner, lax.rem(me + k, n)).start()
            for i in range(hpo):
                ag_recv[my_owner * hpo + i] = ag_send[i]

        if stride == 1:
            attend()
        else:
            pl.when(is_owner)(attend)

        other_owners(lambda owner: ag_copy(owner, me).wait_recv())

        mixes = []
        zero = jnp.zeros((2 * dh, 2 * groups), BF16)
        for p in range(heads // 2):
            even = ag_recv[2 * p]
            odd = ag_recv[2 * p + 1]
            block = jnp.concatenate(
                [
                    jnp.where(lane, even, 0.0),
                    jnp.where(lane, pltpu.roll(even, groups, 1), 0.0),
                    jnp.where(lane, 0.0, pltpu.roll(odd, groups, 1)),
                    jnp.where(lane, 0.0, odd),
                ],
                0,
            ).astype(BF16)
            mixes.append(
                dot(wt[slot, 0, :, 2 * p * dh : 2 * (p + 1) * dh], block).astype(BF16)
            )
        mix = jnp.concatenate(mixes, 1)
        base, wide, hid = {}, {}, {}

        def stage(name, c):
            if not 0 <= c < chunks:
                return
            at = cols_of(c)
            if name == "mix":
                base[c] = stream[:, at] + dot(mix, wts[:, at])
            elif name == "widen":
                wide[c] = dot(wt[slot, 1], norm_columns(base[c]))
            elif name == "gelu":
                hid[c] = gelu(wide[c]).astype(BF16)
            elif name == "contract":
                s = base[c] + dot(wt[slot, 2], hid[c])
                stream[:, at] = s
                normed[:, at] = norm_columns(s)

        for t in range(chunks + 3):
            stage("mix", t)
            stage("gelu", t - 2)
            stage("widen", t - 1)
            stage("contract", t - 2)

        other_owners(lambda owner: rs_copy(owner, me).wait_send())

        def sent():
            for k in range(1, n):
                ag_copy(my_owner, lax.rem(me + k, n)).wait_send()

        if stride == 1:
            sent()
        else:
            pl.when(is_owner)(sent)
        return carry

    def prepare_next(l):
        prepare(l + 1)

    lax.fori_loop(0, layers, layer, 0)

    for c in range(chunks):
        at = slice(c * chunk, (c + 1) * chunk)
        out_ref[:, at] = jnp.where(live(c), stream[:, at], 0.0).astype(BF16)


def per_device(n, x, tally, wv, wp, aff, sharp, ask, match, cont, wo, ww, wc):
    points, feats = x.shape
    layers, heads, dh, groups = aff.shape
    owners = min(n, heads)
    hpo = heads // owners
    quads = max(1, heads // 4)
    chunk = min(points, 256)
    vmem = pl.BlockSpec(memory_space=pltpu.VMEM)
    smem = pl.BlockSpec(memory_space=pltpu.SMEM)
    hbm = pl.BlockSpec(memory_space=pl.ANY)
    dma = pltpu.SemaphoreType.DMA
    turned = pl.pallas_call(
        functools.partial(kernel, n, chunk),
        out_shape=jax.ShapeDtypeStruct((feats, points), BF16),
        in_specs=[smem, smem, hbm] + [vmem] * 4 + [hbm] * 5,
        out_specs=vmem,
        scratch_shapes=[
            pltpu.VMEM(wv.shape, BF16),
            pltpu.VMEM(wp.shape, BF16),
            pltpu.VMEM(wo.shape, BF16),
            pltpu.VMEM(ww.shape, BF16),
            pltpu.VMEM(wc.shape, BF16),
            pltpu.VMEM((feats, points), F32),
            pltpu.VMEM((feats, points), BF16),
            pltpu.VMEM((heads * groups, points), BF16),
            pltpu.VMEM((quads, heads // quads * dh + 16, points), BF16),
            pltpu.VMEM((quads, heads // quads * (groups + dh), feats), BF16),
            pltpu.VMEM((2, 3) + wv.shape[1:], BF16),
            pltpu.VMEM(x.shape, BF16),
            pltpu.VMEM((2, dh, dh), F32),
            pltpu.VMEM((heads, dh // 2 + 8, 2 * groups), F32),
            pltpu.VMEM((n, hpo, dh // 2 + 8, 2 * groups), F32),
            pltpu.VMEM((hpo, dh // 2, 2 * groups), F32),
            pltpu.VMEM((heads, dh // 2, 2 * groups), F32),
            dma((points // chunk,)),
            dma((5, layers)),
            dma((owners,)),
            dma((n,)),
            dma((n,)),
            dma((owners,)),
        ],
        compiler_params=pltpu.CompilerParams(
            collective_id=0, has_side_effects=True, vmem_limit_bytes=60 * 1024 * 1024
        ),
    )(tally, sharp, x, aff, ask, match, cont, wv, wp, wo, ww, wc)
    return turned.T


def solution(mesh):
    rows = P(("batch", "pts"), None)
    placed = (rows, P(("batch", "pts"))) + (P(),) * 10
    return jax.shard_map(
        functools.partial(per_device, mesh.shape["pts"]),
        mesh=mesh,
        in_specs=placed,
        out_specs=rows,
        check_vma=False,
    )
```
